512 devices in a mesh: win: 64 (over z_hi, y, core), head: 8 (over x, z_lo).
Axes of the slice: x: 4, y: 8, z: 8 (z_hi: 4, z_lo: 2; z = z_hi * 2 + z_lo), core: 2. Of those that a mesh axis runs over, the one named last changes fastest.
Arguments:
- qkv: bfloat16 [3, 64, 96, 48, 1024], P(None, 'win', 'head'), may hold values from -10 to 10
Outputs:
- attended: bfloat16 [64, 96, 48, 1024], P('win', 'head')
The draws below stay inside these ranges and needn't reach their ends.
All inputs are finite; a program needn't handle non-finite values.
Results may differ from the reference program's by a relative error of at most 0.0047.
Values may be sent and summed in bfloat16 or wider, within the bound.
No kernel may reach another device: no remote copies, remote signals or barrier semaphores. Data moves between devices by JAX's collectives and lax.ppermute only.
A program may use at most 64 MiB of HBM per device.

```python
import math
import jax
import jax.numpy as jnp
from jax import lax

HEADS = 8
HEAD_DIM = 128
WIN = 48
LAT_WIN = 4
ROWS = 192
HALF_ROWS = 96
LON_BANDS = 32


def draw_qkv(key, part):
    channels = HEADS * HEAD_DIM
    blocks = 2 * LON_BANDS
    full_shape = (3, blocks, HALF_ROWS, WIN, channels)
    key_base = jax.random.fold_in(jax.random.fold_in(key, 7), 0)
    values = jnp.clip(jax.random.normal(key_base, full_shape, jnp.float32), -6.0, 6.0)
    return values.astype(jnp.bfloat16)


def setup_inputs(seed: int = 0) -> dict:
    seeds = jax.random.split(jax.random.key(seed), 2)
    qkv = draw_qkv(jax.random.fold_in(seeds[1], 71), 0)
    return {"qkv": qkv}


def attend(queries, keys, values, labels_query, labels_key):
    score_scale = 1.0 / math.sqrt(queries.shape[-1])
    scores = jnp.einsum('qhd,khd->hqk', queries.astype(jnp.float32), keys.astype(jnp.float32)) * score_scale
    allowed = labels_query[:, None] == labels_key[None, :]
    scores = jnp.where(allowed[None], scores, -jnp.inf)
    row_max = lax.optimization_barrier(jnp.max(scores, axis=-1, keepdims=True))
    weights = jnp.exp(scores - row_max)
    row_total = lax.optimization_barrier(jnp.sum(weights, axis=-1, keepdims=True))
    rounded = lax.optimization_barrier(weights.astype(jnp.bfloat16)).astype(jnp.float32)
    mixture = jnp.einsum('hqk,khd->qhd', rounded, values.astype(jnp.float32))
    return (mixture / jnp.transpose(row_total, (1, 0, 2))).astype(jnp.bfloat16)

def reference(qkv):
    half_cols = WIN // 2
    channels = HEADS * HEAD_DIM
    bands = qkv.reshape(3, LON_BANDS, ROWS, WIN, channels)
    rolled_rows = jnp.roll(jnp.arange(ROWS, dtype=jnp.int32), -half_cols)
    row_labels = (rolled_rows < half_cols).astype(jnp.int32)
    label_parts = jnp.broadcast_to(row_labels.reshape(LAT_WIN, WIN, 1), (LAT_WIN, WIN, WIN)).reshape(LAT_WIN, WIN * WIN)

    def one_window(lon_index):
        east_index = ((lon_index + 1) % LON_BANDS).astype(jnp.int32)
        own_band = lax.dynamic_index_in_dim(bands, lon_index, 1, keepdims=False)
        east_band = lax.dynamic_index_in_dim(bands, east_index, 1, keepdims=False)
        window = jnp.concatenate([own_band[:, :, half_cols:], east_band[:, :, :half_cols]], axis=2)
        window = jnp.roll(window, -half_cols, axis=1)
        window_parts = window.reshape(3, LAT_WIN, WIN * WIN, HEADS, HEAD_DIM)

        def one_band(pieces):
            window_part, label_part = pieces
            return attend(window_part[0], window_part[1], window_part[2], label_part, label_part)
        result = lax.map(one_band, (jnp.moveaxis(window_parts, 1, 0), label_parts))
        result = result.reshape(ROWS, WIN, channels)
        return jnp.roll(result, half_cols, axis=0)
    outputs = lax.map(one_window, jnp.arange(LON_BANDS, dtype=jnp.int32))
    joined = jnp.concatenate([jnp.roll(outputs[:, :, half_cols:], 1, axis=0), outputs[:, :, :half_cols]], axis=2)
    return joined.reshape(2 * LON_BANDS, HALF_ROWS, WIN, channels)
```

```python
import math

import jax
import jax.numpy as jnp
from jax import lax
from jax.experimental import pallas as pl
from jax.experimental.pallas import tpu as pltpu
from jax.sharding import PartitionSpec as P

AXES = ("win", "head")
HEAD_DIM = 128
PEERS = 8


def flat(band, core, x, z_lo):
    return (band * 2 + core) * 8 + x * 2 + z_lo


def members(band, lat):
    out = []
    for late in range(2):
        if lat % 2 == 0:
            x, core = 1 + late, lat // 2
        else:
            x, core = (3, 0)[late], (lat // 2) ^ late
        for side in range(2):
            for z_lo in range(2):
                out.append(flat((band + side) % 32, core, x, z_lo))
    return out


def groups(parity):
    return [members(band, lat) for band in range(parity, 32, 2) for lat in range(4)]


def split_kernel(east_ref, qkv_ref, out_ref, sems):
    half = qkv_ref.shape[2] // 2
    first = pl.multiple_of(east_ref[0] * half, 8)
    copies = []
    for h in range(PEERS):
        copies.append(
            pltpu.make_async_copy(
                qkv_ref.at[:, :, pl.ds(first, half), h * HEAD_DIM : (h + 1) * HEAD_DIM],
                out_ref.at[h],
                sems.at[h],
            )
        )
    for copy in copies:
        copy.start()
    for copy in copies:
        copy.wait()


def split_heads(tokens, east):
    _, rows, cols, _ = tokens.shape
    return pl.pallas_call(
        split_kernel,
        out_shape=jax.ShapeDtypeStruct((PEERS, 3, rows, cols // 2, HEAD_DIM), tokens.dtype),
        in_specs=[
            pl.BlockSpec(memory_space=pltpu.SMEM),
            pl.BlockSpec(memory_space=pl.ANY),
        ],
        out_specs=pl.BlockSpec(memory_space=pl.ANY),
        scratch_shapes=[pltpu.SemaphoreType.DMA((PEERS,))],
        name="split_heads",
    )(east, tokens)


def join_kernel(east_ref, first_ref, second_ref, out_ref, sems):
    half = out_ref.shape[1] // 2
    copies = []
    for parity, blocks in enumerate((first_ref, second_ref)):
        east = east_ref[0] if parity == 0 else 1 - east_ref[0]
        col = pl.multiple_of(east * half, 8)
        for h in range(PEERS):
            copies.append(
                pltpu.make_async_copy(
                    blocks.at[h],
                    out_ref.at[:, pl.ds(col, half), h * HEAD_DIM : (h + 1) * HEAD_DIM],
                    sems.at[parity, h],
                )
            )
    for copy in copies:
        copy.start()
    for copy in copies:
        copy.wait()


def join_heads(east, first, second):
    heads, rows, half, width = first.shape
    return pl.pallas_call(
        join_kernel,
        out_shape=jax.ShapeDtypeStruct((rows, 2 * half, heads * width), first.dtype),
        in_specs=[
            pl.BlockSpec(memory_space=pltpu.SMEM),
            pl.BlockSpec(memory_space=pl.ANY),
            pl.BlockSpec(memory_space=pl.ANY),
        ],
        out_specs=pl.BlockSpec(memory_space=pl.ANY),
        scratch_shapes=[pltpu.SemaphoreType.DMA((2, PEERS))],
        name="join_heads",
    )(east, first, second)


def attend_kernel(split_ref, qkv_ref, out_ref, keys, values):
    blocks, _, count, width = qkv_ref.shape
    scale = 1.0 / math.sqrt(width)
    for b in range(blocks):
        keys[b * count : (b + 1) * count] = qkv_ref[b, 1]
        values[b * count : (b + 1) * count] = qkv_ref[b, 2]
    half = blocks // 2

    def attend(block, low, high):
        scores = lax.dot_general(
            qkv_ref[block, 0],
            keys[low:high],
            (((1,), (1,)), ((), ())),
            preferred_element_type=jnp.float32,
        )
        scores = scores * scale
        row_max = jnp.max(scores, axis=-1, keepdims=True)
        weights = jnp.exp(scores - row_max)
        row_total = jnp.sum(weights, axis=-1, keepdims=True)
        mixture = jnp.dot(
            weights.astype(jnp.bfloat16), values[low:high], preferred_element_type=jnp.float32
        )
        out_ref[block] = (mixture / row_total).astype(out_ref.dtype)

    @pl.when(split_ref[0] == 0)
    def _():
        for block in range(blocks):
            attend(block, 0, blocks * count)

    @pl.when(split_ref[0] != 0)
    def _():
        for block in range(blocks):
            low = 0 if block < half else half * count
            attend(block, low, low + half * count)


def attend(split, qkv):
    blocks, _, count, width = qkv.shape
    return pl.pallas_call(
        attend_kernel,
        out_shape=jax.ShapeDtypeStruct((blocks, count, width), qkv.dtype),
        in_specs=[
            pl.BlockSpec(memory_space=pltpu.SMEM),
            pl.BlockSpec(memory_space=pltpu.VMEM),
        ],
        out_specs=pl.BlockSpec(memory_space=pltpu.VMEM),
        scratch_shapes=[
            pltpu.VMEM((blocks * count, width), qkv.dtype),
            pltpu.VMEM((blocks * count, width), qkv.dtype),
        ],
        compiler_params=pltpu.CompilerParams(vmem_limit_bytes=48 * 2**20),
        name="attend",
    )(split, qkv)


def exchange(blocks, parity):
    return lax.all_to_all(
        blocks, AXES, split_axis=0, concat_axis=0, axis_index_groups=groups(parity), tiled=True
    )


def body(qkv):
    tokens = qkv[:, 0]
    rows, half = tokens.shape[1], tokens.shape[2] // 2
    win, head = lax.axis_index("win"), lax.axis_index("head")
    core, band_odd, x = win % 2, (win // 2) % 2, head // 2
    split = jnp.logical_or(
        jnp.logical_and(x == 3, core == 1), jnp.logical_and(x == 0, core == 0)
    ).astype(jnp.int32)[None]
    arrived = []
    for parity in (1, 0):
        east = (band_odd == parity).astype(jnp.int32)[None]
        arrived.append((parity, exchange(split_heads(tokens, east), parity)))
    outs = {}
    for parity, blocks in arrived:
        result = attend(split, blocks.reshape(PEERS, 3, rows * half, HEAD_DIM))
        outs[parity] = exchange(result.reshape(PEERS, rows, half, HEAD_DIM), parity)
    east_first = (band_odd == 0).astype(jnp.int32)[None]
    return join_heads(east_first, outs[0], outs[1])[None]


def solution(mesh):
    in_specs = (P(None, "win", "head", None, None),)
    out_specs = P("win", "head", None, None)
    return jax.shard_map(body, mesh=mesh, in_specs=in_specs, out_specs=out_specs, check_vma=False)
```

```python
import math

import jax
import jax.numpy as jnp
from jax import lax
from jax.experimental import pallas as pl
from jax.experimental.pallas import tpu as pltpu
from jax.sharding import PartitionSpec as P

AXES = ("win", "head")
HEAD_DIM = 128
PEERS = 8
SIDE = (0, 1, 4, 5)


def flat(band, core, x, z_lo):
    return (band % 32 * 2 + core) * 8 + x * 2 + z_lo


def place(lat, late):
    if lat % 2 == 0:
        return 1 + late, lat // 2
    return (3, 0)[late], (lat // 2) ^ late


def holders(band, lat):
    out = []
    for m in range(PEERS):
        x, core = place(lat, m >> 2)
        out.append(flat(band + (m >> 1 & 1), core, x, m & 1))
    return out


def workers(band, lat):
    if band % 8 != 7:
        return holders(band, lat)
    out = []
    for m in range(PEERS):
        x, core = place(lat, m >> 2)
        run = band // 8 + 1 - (m & 1)
        out.append(flat(run * 8 + (0 if m & 2 else 7), core, x, m & 1))
    return out


def windows(parity):
    return [(band, lat) for band in range(parity, 32, 2) for lat in range(4)]


def to_workers(parity, apart):
    return [
        (holders(*w)[m], workers(*w)[m ^ apart]) for w in windows(parity) for m in range(PEERS)
    ]


def to_holders(parity, apart):
    return [(worker, holder) for holder, worker in to_workers(parity, apart)]


def between_workers(parity, apart):
    return [
        (workers(*w)[m], workers(*w)[m ^ apart]) for w in windows(parity) for m in range(PEERS)
    ]


def exchange(blocks, parity):
    return lax.all_to_all(
        blocks,
        AXES,
        split_axis=0,
        concat_axis=0,
        axis_index_groups=[holders(*w) for w in windows(parity)],
        tiled=True,
    )


def lanes(h):
    start = h * HEAD_DIM
    return pl.ds(start if isinstance(h, int) else pl.multiple_of(start, HEAD_DIM), HEAD_DIM)


def split_even_kernel(east_ref, tokens_ref, out_ref):
    for h in range(PEERS):
        out_ref[h] = tokens_ref[..., lanes(h)]


def split_odd_kernel(where_ref, tokens_ref, *out_refs):
    for k, out_ref in enumerate(out_refs):
        out_ref[...] = tokens_ref[..., lanes(where_ref[1] ^ k)]


def split_even(tokens, east):
    kinds, rows, cols, channels = tokens.shape
    half = cols // 2
    return pl.pallas_call(
        split_even_kernel,
        out_shape=jax.ShapeDtypeStruct((PEERS, kinds, rows, half, HEAD_DIM), tokens.dtype),
        grid_spec=pltpu.PrefetchScalarGridSpec(
            num_scalar_prefetch=1,
            grid=(kinds,),
            in_specs=[pl.BlockSpec((1, rows, half, channels), lambda t, east: (t, 0, east[0], 0))],
            out_specs=pl.BlockSpec(
                (PEERS, 1, rows, half, HEAD_DIM), lambda t, east: (0, t, 0, 0, 0)
            ),
        ),
        name="split_even",
    )(east, tokens)


def split_odd(tokens, where):
    kinds, rows, cols, channels = tokens.shape
    half = cols // 2
    block = jax.ShapeDtypeStruct((kinds, rows, half, HEAD_DIM), tokens.dtype)
    return pl.pallas_call(
        split_odd_kernel,
        out_shape=[block] * PEERS,
        grid_spec=pltpu.PrefetchScalarGridSpec(
            num_scalar_prefetch=1,
            grid=(kinds,),
            in_specs=[
                pl.BlockSpec((1, rows, half, channels), lambda t, where: (t, 0, where[0], 0))
            ],
            out_specs=[pl.BlockSpec((1, rows, half, HEAD_DIM), lambda t, where: (t, 0, 0, 0))]
            * PEERS,
        ),
        name="split_odd",
    )(where, tokens)


def join_kernel(where_ref, even_ref, *refs):
    odd_refs, out_ref = refs[:-1], refs[-1]
    is_odd = pl.program_id(0) == where_ref[0]

    @pl.when(jnp.logical_not(is_odd))
    def _():
        for h in range(PEERS):
            out_ref[..., lanes(h)] = even_ref[h]

    @pl.when(is_odd)
    def _():
        for d, odd_ref in zip(SIDE, odd_refs):
            out_ref[..., lanes(where_ref[1] ^ d)] = odd_ref[0]
            out_ref[..., lanes(where_ref[1] ^ d ^ 2)] = odd_ref[1]


def join_heads(where, even, odd):
    heads, rows, half, width = even.shape

    def whole(shape):
        return pl.BlockSpec(shape, lambda c, where: (0,) * len(shape))

    return pl.pallas_call(
        join_kernel,
        out_shape=jax.ShapeDtypeStruct((rows, 2 * half, heads * width), even.dtype),
        grid_spec=pltpu.PrefetchScalarGridSpec(
            num_scalar_prefetch=1,
            grid=(2,),
            in_specs=[whole(even.shape)] + [whole(o.shape) for o in odd],
            out_specs=pl.BlockSpec((rows, half, heads * width), lambda c, where: (0, c, 0)),
        ),
        name="join_heads",
    )(where, even, *odd)


def attend_blocks(split_ref, blocks, outs, keys, values):
    count, width = blocks[0].shape[1:]
    scale = 1.0 / math.sqrt(width)
    for b, block in enumerate(blocks):
        keys[b * count : (b + 1) * count] = block[1]
        values[b * count : (b + 1) * count] = block[2]
    half = len(blocks) // 2

    def attend_one(b, low, high):
        scores = lax.dot_general(
            blocks[b][0],
            keys[low:high],
            (((1,), (1,)), ((), ())),
            preferred_element_type=jnp.float32,
        )
        scores = scores * scale
        row_max = jnp.max(scores, axis=-1, keepdims=True)
        weights = jnp.exp(scores - row_max)
        row_total = jnp.sum(weights, axis=-1, keepdims=True)
        mixture = jnp.dot(
            weights.astype(jnp.bfloat16), values[low:high], preferred_element_type=jnp.float32
        )
        outs[b][...] = (mixture / row_total).astype(outs[b].dtype)

    @pl.when(split_ref[0] == 0)
    def _():
        for b in range(len(blocks)):
            attend_one(b, 0, len(blocks) * count)

    @pl.when(split_ref[0] != 0)
    def _():
        for b in range(len(blocks)):
            low = 0 if b < half else half * count
            attend_one(b, low, low + half * count)


def attend_even_kernel(split_ref, qkv_ref, out_ref, keys, values):
    attend_blocks(
        split_ref,
        [qkv_ref.at[b] for b in range(PEERS)],
        [out_ref.at[b] for b in range(PEERS)],
        keys,
        values,
    )


def attend_odd_kernel(split_ref, *refs):
    blocks, (own_ref, other_ref, keys, values) = refs[:PEERS], refs[PEERS:]
    outs = [None] * PEERS
    for i, d in enumerate(SIDE):
        outs[d], outs[d ^ 2] = own_ref.at[i], other_ref.at[i]
    attend_blocks(split_ref, blocks, outs, keys, values)


def attend(kernel, name, split, operands, out_shape):
    count, width = operands[0].shape[-2:]
    vmem = pl.BlockSpec(memory_space=pltpu.VMEM)
    return pl.pallas_call(
        kernel,
        out_shape=out_shape,
        in_specs=[pl.BlockSpec(memory_space=pltpu.SMEM)] + [vmem] * len(operands),
        out_specs=jax.tree.map(lambda _: vmem, out_shape),
        scratch_shapes=[pltpu.VMEM((PEERS * count, width), operands[0].dtype)] * 2,
        compiler_params=pltpu.CompilerParams(vmem_limit_bytes=48 * 2**20),
        name=name,
    )(split, *operands)


def body(qkv):
    tokens = qkv[:, 0]
    rows, half = tokens.shape[1], tokens.shape[2] // 2
    count = rows * half
    win, head = lax.axis_index("win"), lax.axis_index("head")
    core, band_odd, x, z_lo = win & 1, (win >> 1) & 1, head >> 1, head & 1
    late = ((x == 2) | (x == 0)).astype(jnp.int32)
    member = late * 4 + (1 - band_odd) * 2 + z_lo
    where = jnp.stack([band_odd, member])
    east = (1 - band_odd)[None]
    split = (((x == 3) & (core == 1)) | ((x == 0) & (core == 0))).astype(jnp.int32)[None]

    even = exchange(split_even(tokens, east), 0)
    odd = split_odd(tokens, where)
    odd = [lax.ppermute(odd[k], AXES, to_workers(1, k)) for k in range(PEERS)]

    result = attend(
        attend_even_kernel,
        "attend_even",
        split,
        [even.reshape(PEERS, 3, count, HEAD_DIM)],
        jax.ShapeDtypeStruct((PEERS, count, HEAD_DIM), qkv.dtype),
    )
    even = exchange(result.reshape(PEERS, rows, half, HEAD_DIM), 0)

    own, other = attend(
        attend_odd_kernel,
        "attend_odd",
        split,
        [o.reshape(3, count, HEAD_DIM) for o in odd],
        [jax.ShapeDtypeStruct((4, count, HEAD_DIM), qkv.dtype)] * 2,
    )
    other = lax.ppermute(other, AXES, between_workers(1, 2))
    odd = []
    for i, d in enumerate(SIDE):
        pair = jnp.stack([own[i], other[i]]).reshape(2, rows, half, HEAD_DIM)
        odd.append(lax.ppermute(pair, AXES, to_holders(1, d)))
    return join_heads(where, even, odd)[None]


def solution(mesh):
    in_specs = (P(None, "win", "head", None, None),)
    out_specs = P("win", "head", None, None)
    return jax.shard_map(body, mesh=mesh, in_specs=in_specs, out_specs=out_specs, check_vma=False)
```

```python
import math

import jax
import jax.numpy as jnp
from jax import lax
from jax.experimental import pallas as pl
from jax.experimental.pallas import tpu as pltpu
from jax.sharding import PartitionSpec as P

AXES = ("win", "head")
HEAD_DIM = 128
PEERS = 8
ORDER = (4, 1, 2, 5, 6, 3, 7, 0)
SIDE = (4, 1, 5, 0)


def flat(band, core, x, z_lo):
    return (band % 32 * 2 + core) * 8 + x * 2 + z_lo


def place(lat, late):
    if lat % 2 == 0:
        return 1 + late, lat // 2
    return (3, 0)[late], (lat // 2) ^ late


def holders(band, lat):
    out = []
    for m in range(PEERS):
        x, core = place(lat, m >> 2)
        out.append(flat(band + (m >> 1 & 1), core, x, m & 1))
    return out


def workers(band, lat):
    if band % 8 != 7:
        return holders(band, lat)
    out = []
    for m in range(PEERS):
        x, core = place(lat, m >> 2)
        run = band // 8 + 1 - (m & 1)
        out.append(flat(run * 8 + (0 if m & 2 else 7), core, x, m & 1))
    return out


def windows(parity):
    return [(band, lat) for band in range(parity, 32, 2) for lat in range(4)]


def to_workers(parity, apart):
    return [
        (holders(*w)[m], workers(*w)[m ^ apart]) for w in windows(parity) for m in range(PEERS)
    ]


def to_holders(parity, apart):
    return [(worker, holder) for holder, worker in to_workers(parity, apart)]


def between_workers(parity, apart):
    return [
        (workers(*w)[m], workers(*w)[m ^ apart]) for w in windows(parity) for m in range(PEERS)
    ]


def exchange(blocks, parity):
    return lax.all_to_all(
        blocks,
        AXES,
        split_axis=0,
        concat_axis=0,
        axis_index_groups=[holders(*w) for w in windows(parity)],
        tiled=True,
    )


def lanes(h):
    start = h * HEAD_DIM
    return pl.ds(start if isinstance(h, int) else pl.multiple_of(start, HEAD_DIM), HEAD_DIM)


def split_even_kernel(where_ref, tokens_ref, out_ref):
    for h in range(PEERS):
        out_ref[h] = tokens_ref[..., lanes(h)]


def split_odd_kernel(where_ref, tokens_ref, *out_refs):
    for k, out_ref in enumerate(out_refs):
        out_ref[...] = tokens_ref[..., lanes(where_ref[1] ^ k)]


def cut(kernel, name, where, tokens, odd, out_shape):
    kinds, rows, cols, channels = tokens.shape
    vmem = pl.BlockSpec(memory_space=pltpu.VMEM)
    return pl.pallas_call(
        kernel,
        out_shape=out_shape,
        grid_spec=pltpu.PrefetchScalarGridSpec(
            num_scalar_prefetch=1,
            grid=(1,),
            in_specs=[
                pl.BlockSpec(
                    (kinds, rows, cols // 2, channels),
                    lambda t, where: (0, 0, where[0] if odd else 1 - where[0], 0),
                )
            ],
            out_specs=jax.tree.map(lambda _: vmem, out_shape),
        ),
        compiler_params=pltpu.CompilerParams(vmem_limit_bytes=32 * 2**20),
        name=name,
    )(where, tokens)


def join_kernel(where_ref, even_ref, *refs):
    odd_refs, out_ref = refs[:-1], refs[-1]
    is_odd = pl.program_id(0) == where_ref[0]

    @pl.when(jnp.logical_not(is_odd))
    def _():
        for h in range(PEERS):
            out_ref[..., lanes(h)] = even_ref[h]

    @pl.when(is_odd)
    def _():
        for d, odd_ref in zip(SIDE, odd_refs):
            out_ref[..., lanes(where_ref[1] ^ d)] = odd_ref[0]
            out_ref[..., lanes(where_ref[1] ^ d ^ 2)] = odd_ref[1]


def join_heads(where, even, odd):
    heads, rows, half, width = even.shape

    def whole(shape):
        return pl.BlockSpec(shape, lambda c, where: (0,) * len(shape))

    return pl.pallas_call(
        join_kernel,
        out_shape=jax.ShapeDtypeStruct((rows, 2 * half, heads * width), even.dtype),
        grid_spec=pltpu.PrefetchScalarGridSpec(
            num_scalar_prefetch=1,
            grid=(2,),
            in_specs=[whole(even.shape)] + [whole(o.shape) for o in odd],
            out_specs=pl.BlockSpec((rows, half, heads * width), lambda c, where: (0, c, 0)),
        ),
        name="join_heads",
    )(where, even, *odd)


def attend_blocks(split_ref, blocks, outs, keys, values):
    count, width = blocks[0].shape[1:]
    scale = math.log2(math.e) / math.sqrt(width)
    for b, block in enumerate(blocks):
        keys[b * count : (b + 1) * count] = block[1]
        values[b * count : (b + 1) * count, :width] = block[2]
    values[:, width:] = jnp.ones((values.shape[0], values.shape[1] - width), values.dtype)
    half = len(blocks) // 2

    def attend_one(b, low, high):
        scores = lax.dot_general(
            blocks[b][0],
            keys[low:high],
            (((1,), (1,)), ((), ())),
            preferred_element_type=jnp.float32,
        )
        row_max = jnp.max(scores, axis=-1, keepdims=True)
        weights = jnp.exp2(scores * scale - row_max * scale)
        mixture = jnp.dot(
            weights.astype(jnp.bfloat16), values[low:high], preferred_element_type=jnp.float32
        )
        outs[b][...] = (mixture[:, :width] / mixture[:, width:]).astype(outs[b].dtype)

    @pl.when(split_ref[0] == 0)
    def _():
        for b in range(len(blocks)):
            attend_one(b, 0, len(blocks) * count)

    @pl.when(split_ref[0] != 0)
    def _():
        for b in range(len(blocks)):
            low = 0 if b < half else half * count
            attend_one(b, low, low + half * count)


def attend_even_kernel(split_ref, qkv_ref, out_ref, keys, values):
    attend_blocks(
        split_ref,
        [qkv_ref.at[b] for b in range(PEERS)],
        [out_ref.at[b] for b in range(PEERS)],
        keys,
        values,
    )


def attend_odd_kernel(split_ref, *refs):
    arrived, (own_ref, other_ref, keys, values) = refs[:PEERS], refs[PEERS:]
    blocks, outs = [None] * PEERS, [None] * PEERS
    for k, block in zip(ORDER, arrived):
        blocks[k] = block
    for i, d in enumerate(SIDE):
        outs[d], outs[d ^ 2] = own_ref.at[i], other_ref.at[i]
    attend_blocks(split_ref, blocks, outs, keys, values)


def attend(kernel, name, split, operands, out_shape):
    count, width = operands[0].shape[-2:]
    vmem = pl.BlockSpec(memory_space=pltpu.VMEM)
    return pl.pallas_call(
        kernel,
        out_shape=out_shape,
        in_specs=[pl.BlockSpec(memory_space=pltpu.SMEM)] + [vmem] * len(operands),
        out_specs=jax.tree.map(lambda _: vmem, out_shape),
        scratch_shapes=[
            pltpu.VMEM((PEERS * count, width), operands[0].dtype),
            pltpu.VMEM((PEERS * count, 2 * width), operands[0].dtype),
        ],
        compiler_params=pltpu.CompilerParams(vmem_limit_bytes=48 * 2**20),
        name=name,
    )(split, *operands)


def body(qkv):
    tokens = qkv[:, 0]
    rows, half = tokens.shape[1], tokens.shape[2] // 2
    count = rows * half
    win, head = lax.axis_index("win"), lax.axis_index("head")
    core, band_odd, x, z_lo = win & 1, (win >> 1) & 1, head >> 1, head & 1
    late = ((x == 2) | (x == 0)).astype(jnp.int32)
    member = late * 4 + (1 - band_odd) * 2 + z_lo
    split = (((x == 3) & (core == 1)) | ((x == 0) & (core == 0))).astype(jnp.int32)
    where = jnp.stack([band_odd, member])
    split = split[None]
    block = jax.ShapeDtypeStruct((3, rows, half, HEAD_DIM), qkv.dtype)

    even = jax.ShapeDtypeStruct((PEERS,) + block.shape, qkv.dtype)
    even = cut(split_even_kernel, "split_even", where, tokens, False, even)
    even = exchange(even, 0)
    odd = cut(split_odd_kernel, "split_odd", where, tokens, True, [block] * PEERS)
    odd = [lax.ppermute(odd[k], AXES, to_workers(1, k)) for k in ORDER]

    even = attend(
        attend_even_kernel,
        "attend_even",
        split,
        [even.reshape(PEERS, 3, count, HEAD_DIM)],
        jax.ShapeDtypeStruct((PEERS, count, HEAD_DIM), qkv.dtype),
    )
    even, odd = lax.optimization_barrier((even, odd))
    even = exchange(even.reshape(PEERS, rows, half, HEAD_DIM), 0)

    own, other = attend(
        attend_odd_kernel,
        "attend_odd",
        split,
        [o.reshape(3, count, HEAD_DIM) for o in odd],
        [jax.ShapeDtypeStruct((4, count, HEAD_DIM), qkv.dtype)] * 2,
    )
    other = lax.ppermute(other, AXES, between_workers(1, 2))
    odd = []
    for i, d in enumerate(SIDE):
        pair = jnp.stack([own[i], other[i]]).reshape(2, rows, half, HEAD_DIM)
        odd.append(lax.ppermute(pair, AXES, to_holders(1, d)))
    return join_heads(where, even, odd)[None]


def solution(mesh):
    in_specs = (P(None, "win", "head", None, None),)
    out_specs = P("win", "head", None, None)
    return jax.shard_map(body, mesh=mesh, in_specs=in_specs, out_specs=out_specs, check_vma=False)
```

```python
import math

import jax
import jax.numpy as jnp
from jax import lax
from jax.experimental import pallas as pl
from jax.experimental.pallas import tpu as pltpu
from jax.sharding import PartitionSpec as P

AXES = ("win", "head")
HEAD_DIM = 128
PEERS = 8
ORDER = (2, 1, 4, 3, 6, 5, 7, 0)
SIDE = (4, 1, 5, 0)


def flat(band, core, x, z_lo):
    return (band % 32 * 2 + core) * 8 + x * 2 + z_lo


def place(lat, late):
    if lat % 2 == 0:
        return 1 + late, lat // 2
    return (3, 0)[late], (lat // 2) ^ late


def holders(band, lat):
    out = []
    for m in range(PEERS):
        x, core = place(lat, m >> 2)
        out.append(flat(band + (m >> 1 & 1), core, x, m & 1))
    return out


def workers(band, lat):
    if band % 8 != 7:
        return holders(band, lat)
    out = []
    for m in range(PEERS):
        x, core = place(lat, m >> 2)
        run = band // 8 + 1 - (m & 1)
        out.append(flat(run * 8 + (0 if m & 2 else 7), core, x, m & 1))
    return out


def windows(parity):
    return [(band, lat) for band in range(parity, 32, 2) for lat in range(4)]


def to_workers(parity, apart):
    return [
        (holders(*w)[m], workers(*w)[m ^ apart]) for w in windows(parity) for m in range(PEERS)
    ]


def to_holders(parity, apart):
    return [(worker, holder) for holder, worker in to_workers(parity, apart)]


def between_workers(parity, apart):
    return [
        (workers(*w)[m], workers(*w)[m ^ apart]) for w in windows(parity) for m in range(PEERS)
    ]


def exchange(blocks, parity):
    return lax.all_to_all(
        blocks,
        AXES,
        split_axis=0,
        concat_axis=0,
        axis_index_groups=[holders(*w) for w in windows(parity)],
        tiled=True,
    )


def lanes(h):
    start = h * HEAD_DIM
    return pl.ds(start if isinstance(h, int) else pl.multiple_of(start, HEAD_DIM), HEAD_DIM)


def split_even_kernel(where_ref, tokens_ref, out_ref):
    for h in range(PEERS):
        out_ref[h] = tokens_ref[..., lanes(h)]


def split_odd_kernel(where_ref, tokens_ref, *out_refs):
    for k, out_ref in enumerate(out_refs):
        out_ref[...] = tokens_ref[..., lanes(where_ref[1] ^ k)]


def cut(kernel, name, where, tokens, odd, out_shape):
    kinds, rows, cols, channels = tokens.shape
    vmem = pl.BlockSpec(memory_space=pltpu.VMEM)
    return pl.pallas_call(
        kernel,
        out_shape=out_shape,
        grid_spec=pltpu.PrefetchScalarGridSpec(
            num_scalar_prefetch=1,
            grid=(1,),
            in_specs=[
                pl.BlockSpec(
                    (kinds, rows, cols // 2, channels),
                    lambda t, where: (0, 0, where[0] if odd else 1 - where[0], 0),
                )
            ],
            out_specs=jax.tree.map(lambda _: vmem, out_shape),
        ),
        compiler_params=pltpu.CompilerParams(vmem_limit_bytes=32 * 2**20),
        name=name,
    )(where, tokens)


def join_kernel(where_ref, even_ref, *refs):
    odd_refs, out_ref = refs[:-1], refs[-1]
    is_odd = pl.program_id(0) == where_ref[0]

    @pl.when(jnp.logical_not(is_odd))
    def _():
        for h in range(PEERS):
            out_ref[..., lanes(h)] = even_ref[h]

    @pl.when(is_odd)
    def _():
        for d, odd_ref in zip(SIDE, odd_refs):
            out_ref[..., lanes(where_ref[1] ^ d)] = odd_ref[0]
            out_ref[..., lanes(where_ref[1] ^ d ^ 2)] = odd_ref[1]


def join_heads(where, even, odd):
    heads, rows, half, width = even.shape

    def whole(shape):
        return pl.BlockSpec(shape, lambda c, where: (0,) * len(shape))

    return pl.pallas_call(
        join_kernel,
        out_shape=jax.ShapeDtypeStruct((rows, 2 * half, heads * width), even.dtype),
        grid_spec=pltpu.PrefetchScalarGridSpec(
            num_scalar_prefetch=1,
            grid=(2,),
            in_specs=[whole(even.shape)] + [whole(o.shape) for o in odd],
            out_specs=pl.BlockSpec((rows, half, heads * width), lambda c, where: (0, c, 0)),
        ),
        name="join_heads",
    )(where, even, *odd)


def attend_blocks(split_ref, blocks, outs, keys, values):
    count, width = blocks[0].shape[1:]
    scale = math.log2(math.e) / math.sqrt(width)
    for b, block in enumerate(blocks):
        keys[b * count : (b + 1) * count] = block[1]
        values[b * count : (b + 1) * count, :width] = block[2]
    values[:, width:] = jnp.ones((values.shape[0], values.shape[1] - width), values.dtype)
    half = len(blocks) // 2

    def attend_one(b, low, high):
        scores = lax.dot_general(
            blocks[b][0],
            keys[low:high],
            (((1,), (1,)), ((), ())),
            preferred_element_type=jnp.float32,
        )
        row_max = jnp.max(scores, axis=-1, keepdims=True)
        weights = jnp.exp2(scores * scale - row_max * scale)
        mixture = jnp.dot(
            weights.astype(jnp.bfloat16), values[low:high], preferred_element_type=jnp.float32
        )
        outs[b][...] = (mixture[:, :width] / mixture[:, width:]).astype(outs[b].dtype)

    @pl.when(split_ref[0] == 0)
    def _():
        for b in range(len(blocks)):
            attend_one(b, 0, len(blocks) * count)

    @pl.when(split_ref[0] != 0)
    def _():
        for b in range(len(blocks)):
            low = 0 if b < half else half * count
            attend_one(b, low, low + half * count)


def attend_even_kernel(split_ref, qkv_ref, out_ref, keys, values):
    attend_blocks(
        split_ref,
        [qkv_ref.at[b] for b in range(PEERS)],
        [out_ref.at[b] for b in range(PEERS)],
        keys,
        values,
    )


def attend_odd_kernel(split_ref, *refs):
    arrived, (own_ref, other_ref, keys, values) = refs[:PEERS], refs[PEERS:]
    blocks, outs = [None] * PEERS, [None] * PEERS
    for k, block in zip(ORDER, arrived):
        blocks[k] = block
    for i, d in enumerate(SIDE):
        outs[d], outs[d ^ 2] = own_ref.at[i], other_ref.at[i]
    attend_blocks(split_ref, blocks, outs, keys, values)


def attend(kernel, name, split, operands, out_shape):
    count, width = operands[0].shape[-2:]
    vmem = pl.BlockSpec(memory_space=pltpu.VMEM)
    return pl.pallas_call(
        kernel,
        out_shape=out_shape,
        in_specs=[pl.BlockSpec(memory_space=pltpu.SMEM)] + [vmem] * len(operands),
        out_specs=jax.tree.map(lambda _: vmem, out_shape),
        scratch_shapes=[
            pltpu.VMEM((PEERS * count, width), operands[0].dtype),
            pltpu.VMEM((PEERS * count, 2 * width), operands[0].dtype),
        ],
        compiler_params=pltpu.CompilerParams(vmem_limit_bytes=48 * 2**20),
        name=name,
    )(split, *operands)


def body(qkv):
    tokens = qkv[:, 0]
    rows, half = tokens.shape[1], tokens.shape[2] // 2
    count = rows * half
    win, head = lax.axis_index("win"), lax.axis_index("head")
    core, band_odd, x, z_lo = win & 1, (win >> 1) & 1, head >> 1, head & 1
    late = ((x == 2) | (x == 0)).astype(jnp.int32)
    member = late * 4 + (1 - band_odd) * 2 + z_lo
    split = (((x == 3) & (core == 1)) | ((x == 0) & (core == 0))).astype(jnp.int32)
    where = jnp.stack([band_odd, member])
    split = split[None]
    block = jax.ShapeDtypeStruct((3, rows, half, HEAD_DIM), qkv.dtype)

    even = jax.ShapeDtypeStruct((PEERS,) + block.shape, qkv.dtype)
    even = cut(split_even_kernel, "split_even", where, tokens, False, even)
    even = exchange(even, 0)
    odd = cut(split_odd_kernel, "split_odd", where, tokens, True, [block] * PEERS)
    odd = [lax.ppermute(odd[k], AXES, to_workers(1, k)) for k in ORDER]

    even = attend(
        attend_even_kernel,
        "attend_even",
        split,
        [even.reshape(PEERS, 3, count, HEAD_DIM)],
        jax.ShapeDtypeStruct((PEERS, count, HEAD_DIM), qkv.dtype),
    )
    even, odd = lax.optimization_barrier((even, odd))
    even = exchange(even.reshape(PEERS, rows, half, HEAD_DIM), 0)

    own, other = attend(
        attend_odd_kernel,
        "attend_odd",
        split,
        [o.reshape(3, count, HEAD_DIM) for o in odd],
        [jax.ShapeDtypeStruct((4, count, HEAD_DIM), qkv.dtype)] * 2,
    )
    other = lax.ppermute(other, AXES, between_workers(1, 2))
    odd = []
    for i, d in enumerate(SIDE):
        pair = jnp.stack([own[i], other[i]]).reshape(2, rows, half, HEAD_DIM)
        odd.append(lax.ppermute(pair, AXES, to_holders(1, d)))
    return join_heads(where, even, odd)[None]


def solution(mesh):
    in_specs = (P(None, "win", "head", None, None),)
    out_specs = P("win", "head", None, None)
    return jax.shard_map(body, mesh=mesh, in_specs=in_specs, out_specs=out_specs, check_vma=False)
```

```python
import math

import jax
import jax.numpy as jnp
from jax import lax
from jax.experimental import pallas as pl
from jax.experimental.pallas import tpu as pltpu
from jax.sharding import PartitionSpec as P

AXES = ("win", "head")
HEAD_DIM = 128
PEERS = 8
ORDER = (2, 1, 4, 3, 6, 5, 7, 0)
SIDE = (5, 1, 4, 0)


def flat(band, core, x, z_lo):
    return (band % 32 * 2 + core) * 8 + x * 2 + z_lo


def place(lat, late):
    if lat % 2 == 0:
        return 1 + late, lat // 2
    return (3, 0)[late], (lat // 2) ^ late


def holders(band, lat):
    out = []
    for m in range(PEERS):
        x, core = place(lat, m >> 2)
        out.append(flat(band + (m >> 1 & 1), core, x, m & 1))
    return out


def workers(band, lat):
    if band % 8 != 7:
        return holders(band, lat)
    out = []
    for m in range(PEERS):
        x, core = place(lat, m >> 2)
        run = band // 8 + 1 - (m & 1)
        out.append(flat(run * 8 + (0 if m & 2 else 7), core, x, m & 1))
    return out


def windows(parity):
    return [(band, lat) for band in range(parity, 32, 2) for lat in range(4)]


def to_workers(parity, apart):
    return [
        (holders(*w)[m], workers(*w)[m ^ apart]) for w in windows(parity) for m in range(PEERS)
    ]


def to_holders(parity, apart):
    return [(worker, holder) for holder, worker in to_workers(parity, apart)]


def between_workers(parity, apart):
    return [
        (workers(*w)[m], workers(*w)[m ^ apart]) for w in windows(parity) for m in range(PEERS)
    ]


def exchange(blocks, parity):
    return lax.all_to_all(
        blocks,
        AXES,
        split_axis=0,
        concat_axis=0,
        axis_index_groups=[holders(*w) for w in windows(parity)],
        tiled=True,
    )


def lanes(h):
    start = h * HEAD_DIM
    return pl.ds(start if isinstance(h, int) else pl.multiple_of(start, HEAD_DIM), HEAD_DIM)


def split_even_kernel(where_ref, tokens_ref, out_ref):
    for h in range(PEERS):
        out_ref[h] = tokens_ref[..., lanes(h)]


def split_odd_kernel(where_ref, tokens_ref, *out_refs):
    for k, out_ref in enumerate(out_refs):
        out_ref[...] = tokens_ref[..., lanes(where_ref[1] ^ k)]


def cut(kernel, name, where, tokens, odd, out_shape):
    kinds, rows, cols, channels = tokens.shape
    vmem = pl.BlockSpec(memory_space=pltpu.VMEM)
    return pl.pallas_call(
        kernel,
        out_shape=out_shape,
        grid_spec=pltpu.PrefetchScalarGridSpec(
            num_scalar_prefetch=1,
            grid=(1,),
            in_specs=[
                pl.BlockSpec(
                    (kinds, rows, cols // 2, channels),
                    lambda t, where: (0, 0, where[0] if odd else 1 - where[0], 0),
                )
            ],
            out_specs=jax.tree.map(lambda _: vmem, out_shape),
        ),
        compiler_params=pltpu.CompilerParams(vmem_limit_bytes=32 * 2**20),
        name=name,
    )(where, tokens)


def join_kernel(where_ref, even_ref, *refs):
    odd_refs, out_ref = refs[:-1], refs[-1]
    is_odd = pl.program_id(0) == where_ref[0]

    @pl.when(jnp.logical_not(is_odd))
    def _():
        for h in range(PEERS):
            out_ref[..., lanes(h)] = even_ref[h]

    @pl.when(is_odd)
    def _():
        for d, odd_ref in zip(SIDE, odd_refs):
            out_ref[..., lanes(where_ref[1] ^ d)] = odd_ref[0]
            out_ref[..., lanes(where_ref[1] ^ d ^ 2)] = odd_ref[1]


def join_heads(where, even, odd):
    heads, rows, half, width = even.shape

    def whole(shape):
        return pl.BlockSpec(shape, lambda c, where: (0,) * len(shape))

    return pl.pallas_call(
        join_kernel,
        out_shape=jax.ShapeDtypeStruct((rows, 2 * half, heads * width), even.dtype),
        grid_spec=pltpu.PrefetchScalarGridSpec(
            num_scalar_prefetch=1,
            grid=(2,),
            in_specs=[whole(even.shape)] + [whole(o.shape) for o in odd],
            out_specs=pl.BlockSpec((rows, half, heads * width), lambda c, where: (0, c, 0)),
        ),
        name="join_heads",
    )(where, even, *odd)


def attend_blocks(split_ref, blocks, outs, keys, values):
    count, width = blocks[0].shape[1:]
    scale = math.log2(math.e) / math.sqrt(width)
    for b, block in enumerate(blocks):
        keys[b * count : (b + 1) * count] = block[1]
        values[b * count : (b + 1) * count, :width] = block[2]
    values[:, width:] = jnp.ones((values.shape[0], values.shape[1] - width), values.dtype)
    half = len(blocks) // 2

    def attend_one(b, low, high):
        scores = lax.dot_general(
            blocks[b][0],
            keys[low:high],
            (((1,), (1,)), ((), ())),
            preferred_element_type=jnp.float32,
        )
        row_max = jnp.max(scores, axis=-1, keepdims=True)
        weights = jnp.exp2(scores * scale - row_max * scale)
        mixture = jnp.dot(
            weights.astype(jnp.bfloat16), values[low:high], preferred_element_type=jnp.float32
        )
        outs[b][...] = (mixture[:, :width] / mixture[:, width:]).astype(outs[b].dtype)

    @pl.when(split_ref[0] == 0)
    def _():
        for b in range(len(blocks)):
            attend_one(b, 0, len(blocks) * count)

    @pl.when(split_ref[0] != 0)
    def _():
        for b in range(len(blocks)):
            low = 0 if b < half else half * count
            attend_one(b, low, low + half * count)


def attend_even_kernel(split_ref, qkv_ref, out_ref, keys, values):
    attend_blocks(
        split_ref,
        [qkv_ref.at[b] for b in range(PEERS)],
        [out_ref.at[b] for b in range(PEERS)],
        keys,
        values,
    )


def attend_odd_kernel(split_ref, *refs):
    arrived, (own_ref, other_ref, keys, values) = refs[:PEERS], refs[PEERS:]
    blocks, outs = [None] * PEERS, [None] * PEERS
    for k, block in zip(ORDER, arrived):
        blocks[k] = block
    for i, d in enumerate(SIDE):
        outs[d], outs[d ^ 2] = own_ref.at[i], other_ref.at[i]
    attend_blocks(split_ref, blocks, outs, keys, values)


def attend(kernel, name, split, operands, out_shape):
    count, width = operands[0].shape[-2:]
    vmem = pl.BlockSpec(memory_space=pltpu.VMEM)
    return pl.pallas_call(
        kernel,
        out_shape=out_shape,
        in_specs=[pl.BlockSpec(memory_space=pltpu.SMEM)] + [vmem] * len(operands),
        out_specs=jax.tree.map(lambda _: vmem, out_shape),
        scratch_shapes=[
            pltpu.VMEM((PEERS * count, width), operands[0].dtype),
            pltpu.VMEM((PEERS * count, 2 * width), operands[0].dtype),
        ],
        compiler_params=pltpu.CompilerParams(vmem_limit_bytes=48 * 2**20),
        name=name,
    )(split, *operands)


def body(qkv):
    tokens = qkv[:, 0]
    rows, half = tokens.shape[1], tokens.shape[2] // 2
    count = rows * half
    win, head = lax.axis_index("win"), lax.axis_index("head")
    core, band_odd, x, z_lo = win & 1, (win >> 1) & 1, head >> 1, head & 1
    late = ((x == 2) | (x == 0)).astype(jnp.int32)
    member = late * 4 + (1 - band_odd) * 2 + z_lo
    split = (((x == 3) & (core == 1)) | ((x == 0) & (core == 0))).astype(jnp.int32)
    where = jnp.stack([band_odd, member])
    split = split[None]
    block = jax.ShapeDtypeStruct((3, rows, half, HEAD_DIM), qkv.dtype)

    even = jax.ShapeDtypeStruct((PEERS,) + block.shape, qkv.dtype)
    even = cut(split_even_kernel, "split_even", where, tokens, False, even)
    even = exchange(even, 0)
    odd = cut(split_odd_kernel, "split_odd", where, tokens, True, [block] * PEERS)
    odd = [lax.ppermute(odd[k], AXES, to_workers(1, k)) for k in ORDER]

    even = attend(
        attend_even_kernel,
        "attend_even",
        split,
        [even.reshape(PEERS, 3, count, HEAD_DIM)],
        jax.ShapeDtypeStruct((PEERS, count, HEAD_DIM), qkv.dtype),
    )
    even, odd = lax.optimization_barrier((even, odd))
    even = exchange(even.reshape(PEERS, rows, half, HEAD_DIM), 0)

    own, other = attend(
        attend_odd_kernel,
        "attend_odd",
        split,
        [o.reshape(3, count, HEAD_DIM) for o in odd],
        [jax.ShapeDtypeStruct((4, count, HEAD_DIM), qkv.dtype)] * 2,
    )
    other = lax.ppermute(other, AXES, between_workers(1, 2))
    odd = []
    for i, d in enumerate(SIDE):
        pair = jnp.stack([own[i], other[i]]).reshape(2, rows, half, HEAD_DIM)
        odd.append(lax.ppermute(pair, AXES, to_holders(1, d)))
    return join_heads(where, even, odd)[None]


def solution(mesh):
    in_specs = (P(None, "win", "head", None, None),)
    out_specs = P("win", "head", None, None)
    return jax.shard_map(body, mesh=mesh, in_specs=in_specs, out_specs=out_specs, check_vma=False)
```
